32 devices in a mesh: ctx: 8 (over z, x), fsdp: 4 (over y, core).
Axes of the slice: x: 2, y: 2, z: 4, core: 2. Of those that a mesh axis runs over, the one named last changes fastest.
Arguments:
- inputs: bfloat16 [4, 1024, 1024], P('fsdp', 'ctx'), may hold values from -6 to 6
- segment_ids: int32 [4, 1024], P('fsdp', 'ctx'), may hold values from 0 to 1, never falling along the last dimension, each value on 1 to 768 neighbouring positions
- gain_attn: bfloat16 [1024], P(('ctx', 'fsdp')), may hold values from 0.5 to 1.5
- w_qkv: bfloat16 [1024, 3072], P(('ctx', 'fsdp')), may hold values from -4 to 4
- w_out_attn: bfloat16 [1024, 1024], P(('ctx', 'fsdp')), may hold values from -1.5 to 1.5
- gain_mlp: bfloat16 [1024], P(('ctx', 'fsdp')), may hold values from 0.5 to 1.5
- w_in: bfloat16 [1024, 5248], P(('ctx', 'fsdp')), may hold values from -0.1875 to 0.1875
- w_out_mlp: bfloat16 [2624, 1024], P(None, ('ctx', 'fsdp')), may hold values from -0.125 to 0.125
- cotangent: bfloat16 [4, 1024, 1024], P('fsdp', 'ctx'), may hold values from -6 to 6
Outputs:
- block_out: bfloat16 [4, 1024, 1024], P('fsdp', 'ctx')
- grad_input: bfloat16 [4, 1024, 1024], P('fsdp', 'ctx')
- grad_w_qkv: float32 [1024, 3072], P(('ctx', 'fsdp'))
- grad_w_out_attn: float32 [1024, 1024], P(('ctx', 'fsdp'))
- grad_w_in: float32 [1024, 5248], P(('ctx', 'fsdp'))
- grad_w_out_mlp: float32 [2624, 1024], P(None, ('ctx', 'fsdp'))
- grad_gain_attn: float32 [1024], P(('ctx', 'fsdp'))
- grad_gain_mlp: float32 [1024], P(('ctx', 'fsdp'))
The draws below stay inside these ranges and needn't reach their ends.
Inputs may be any that keep to these rules, and one draw needn't show every extreme that they name: `segment_ids`: along a row the ids never fall: segment 0 comes first, then segment 1; each segment holds 256 to 768 tokens.
All inputs are finite; a program needn't handle non-finite values.
Results may differ from the reference program's by a relative error of at most 0.015.
Values may be sent and summed in bfloat16 or wider, within the bound.
A program may use at most 256 MiB of HBM per device.

```python
import math
import jax
import jax.numpy as jnp
import numpy as np
from jax import lax

D = 1024
HEADS = 16
HD = 64
FF = 2624
SEQ_TOK = 1024
ROWS = 4
SEG_MOST = 768


def draw_w_qkv(key, part):
    base = jax.random.normal(key, (D, 3 * D), jnp.float32) * D ** (-0.5)
    return base.astype(jnp.bfloat16)


def steps_of(stream_key, dims, cuts, least, top_value):
    def one(position, shards_of):
        heights = jax.random.uniform(jax.random.fold_in(jax.random.fold_in(stream_key, 6), position), (shards_of,), jnp.float32, least / len(cuts), top_value / len(cuts))
        return jnp.repeat(jnp.exp(heights), dims[position] // shards_of).reshape((-1,) + (1,) * (len(dims) - position - 1))

    level = one(*cuts[0])
    for cut in cuts[1:]:
        level = level * one(*cut)
    return level


def profile(amount, total, limit, slope):
    weights = [(1 << 20) // math.isqrt(standing ** slope) + 1 for standing in range(2, amount + 1)]
    surplus, given = total - limit - (amount - 1), [1] * (amount - 1)
    while surplus > 0:
        candidates = [i for i in range(amount - 1) if given[i] < limit]
        pool, left = sum([weights[i] for i in candidates]), surplus
        for i in candidates:
            extra = min(limit - given[i], max(1, left * weights[i] // pool), surplus)
            given[i] = given[i] + extra
            surplus = surplus - extra
    return np.array([limit] + given)


def uneven_parts(own_key, count, total, reach, skew):
    if count == 2:
        one = jax.random.randint(own_key, (), max(1, total - reach), min(reach, total - 1) + 1)
        return jnp.stack([one, total - one])
    sizes = jnp.asarray(profile(count, total, reach, skew), jnp.int32)
    pairs = (count - 1) // 2
    giver, sink = sizes[1:1 + 2 * pairs:2], sizes[2:2 + 2 * pairs:2]
    slack = jnp.minimum(giver - 1, reach - sink)
    moved = jax.random.randint(jax.random.fold_in(own_key, 1), (pairs,), 0, 1 << 20) % (slack + 1)
    sizes = sizes.at[1:1 + 2 * pairs:2].set(giver - moved).at[2:2 + 2 * pairs:2].set(sink + moved)
    return sizes[jax.random.permutation(jax.random.fold_in(own_key, 2), count)]


def noise(stream_key, dims, deviation, most, cuts=(), held_as=jnp.bfloat16):
    result = jax.random.normal(stream_key, dims, jnp.float32) * deviation
    if len(cuts) > 0:
        result = steps_of(stream_key, dims, cuts, -0.22, 0.18) * result
    return jnp.clip(result, min=-most, max=most).astype(held_as)


def setup_inputs(seed: int = 0) -> dict:
    keys = jax.random.split(jax.random.key(seed), 10)
    return {
        "inputs": noise(keys[0], (ROWS, SEQ_TOK, D), 1.0, 6.0, ((0, 4), (1, 8))),
        "segment_ids": jax.vmap(lambda own: jnp.searchsorted(jnp.cumsum(uneven_parts(own, 2, SEQ_TOK, SEG_MOST, 0)), jnp.arange(SEQ_TOK), side="right"))(jax.random.split(keys[1], ROWS)).reshape((ROWS, SEQ_TOK)).astype(jnp.int32),
        "gain_attn": jnp.clip(1.0 + 0.1 * jax.random.normal(keys[2], (D,), jnp.float32), 0.5, 1.5).astype(jnp.bfloat16),
        "w_qkv": draw_w_qkv(jax.random.fold_in(keys[9], 71), 0),
        "w_out_attn": noise(keys[4], (D, D), (max(D * 16 // SEQ_TOK, 1)) ** -0.5, 1.5, ((0, 32),)),
        "gain_mlp": jnp.clip(1.0 + 0.1 * jax.random.normal(keys[5], (D,), jnp.float32), 0.5, 1.5).astype(jnp.bfloat16),
        "w_in": noise(keys[6], (D, 2 * FF), D ** -0.5, 0.1875, ((0, 32),)),
        "w_out_mlp": noise(keys[7], (FF, D), FF ** -0.5, 0.125, ((1, 32),)),
        "cotangent": noise(keys[8], (ROWS, SEQ_TOK, D), 1.0, 6.0, ((0, 4), (1, 8))),
    }


EPSILON = 1e-05
ROPE_BASE = 160000.0

def layer_norm(values):
    center = values - lax.optimization_barrier(jnp.mean(values, axis=-1, keepdims=True))
    scaled = lax.rsqrt(lax.optimization_barrier(jnp.mean(center * center, axis=-1, keepdims=True)) + EPSILON)
    return (center * scaled, scaled)

def norm_back(grad_norm, normed, scaled):
    return scaled * (grad_norm - lax.optimization_barrier(jnp.mean(grad_norm, axis=-1, keepdims=True)) - normed * lax.optimization_barrier(jnp.mean(grad_norm * normed, axis=-1, keepdims=True)))

def rope_tables(positions, head_size):
    freqs = ROPE_BASE ** (-jnp.arange(0, head_size, 2, dtype=jnp.float32) / head_size)
    angles = positions[:, None] * freqs[None, :]
    cosine = jnp.concatenate([jnp.cos(angles), jnp.cos(angles)], axis=-1)
    sine = jnp.concatenate([jnp.sin(angles), jnp.sin(angles)], axis=-1)
    return (cosine[:, None, :], sine[:, None, :])

def rotate(values, cosine, sine):
    half = values.shape[-1] // 2
    turned = jnp.concatenate([-values[..., half:], values[..., :half]], axis=-1)
    return values * cosine + turned * sine

def unrotate(grads, cosine, sine):
    half = grads.shape[-1] // 2
    weighted = grads * sine
    turned = jnp.concatenate([weighted[..., half:], -weighted[..., :half]], axis=-1)
    return grads * cosine + turned

def gelu_slope(values):
    return 0.5 * (1.0 + lax.erf(values * 0.7071067811865476)) + values * jnp.exp(-0.5 * values * values) * 0.3989422804014327

def reference(inputs, segment_ids, gain_attn, w_qkv, w_out_attn, gain_mlp, w_in, w_out_mlp, cotangent):
    scale = 1.0 / math.sqrt(HD)
    positions = jnp.arange(SEQ_TOK, dtype=jnp.int32).astype(jnp.float32)
    cosine, sine = rope_tables(positions, HD)
    gain_first = gain_attn.astype(jnp.float32)
    gain_second = gain_mlp.astype(jnp.float32)

    def one_row(carry, row):
        tokens_in, seg_row, grad_out = row
        tokens = tokens_in.astype(jnp.float32)
        same_doc = seg_row[:, None] == seg_row[None, :]
        normed_one, scale_one = layer_norm(tokens)
        normed_attn = (normed_one * gain_first).astype(jnp.bfloat16)
        projected = jnp.dot(normed_attn, w_qkv, preferred_element_type=jnp.float32)
        queries = rotate(projected[:, :D].reshape(SEQ_TOK, HEADS, HD), cosine, sine).astype(jnp.bfloat16)
        keys_rot = rotate(projected[:, D:2 * D].reshape(SEQ_TOK, HEADS, HD), cosine, sine).astype(jnp.bfloat16)
        values_all = projected[:, 2 * D:].astype(jnp.bfloat16).reshape(SEQ_TOK, HEADS, HD)
        query_heads = jnp.transpose(queries, (1, 0, 2))
        key_heads = jnp.transpose(keys_rot, (1, 0, 2))
        value_heads = jnp.transpose(values_all, (1, 0, 2))

        def head_scores(query_head, key_head):
            scores = jnp.dot(query_head, key_head.T, preferred_element_type=jnp.float32) * scale
            return jnp.where(same_doc, scores, -jnp.inf)

        def head_forward(pieces):
            query_head, key_head, value_head = pieces
            scores = head_scores(query_head, key_head)
            peak = lax.optimization_barrier(jnp.max(scores, axis=-1, keepdims=True))
            log_total = peak + jnp.log(lax.optimization_barrier(jnp.sum(jnp.exp(scores - peak), axis=-1, keepdims=True)))
            probs = jnp.exp(scores - log_total).astype(jnp.bfloat16)
            attended = jnp.dot(probs, value_head, preferred_element_type=jnp.float32).astype(jnp.bfloat16)
            return (attended, log_total)
        attended_heads, log_totals = lax.map(head_forward, (query_heads, key_heads, value_heads))
        attended = jnp.transpose(attended_heads, (1, 0, 2)).reshape(SEQ_TOK, D)
        residual = tokens + jnp.dot(attended, w_out_attn, preferred_element_type=jnp.float32)
        normed_two, scale_two = layer_norm(residual)
        normed_mlp = (normed_two * gain_second).astype(jnp.bfloat16)
        expanded = jnp.dot(normed_mlp, w_in, preferred_element_type=jnp.float32)
        pre_act = expanded[:, :FF]
        gate_part = expanded[:, FF:]
        activated = jax.nn.gelu(pre_act, approximate=False)
        product = (activated * gate_part).astype(jnp.bfloat16)
        block_out = (residual + jnp.dot(product, w_out_mlp, preferred_element_type=jnp.float32)).astype(jnp.bfloat16)
        grad_mlp_out = jnp.dot(product.T, grad_out, preferred_element_type=jnp.float32)
        grad_product = jnp.dot(grad_out, w_out_mlp.T, preferred_element_type=jnp.float32)
        grad_expanded = jnp.concatenate([grad_product * gate_part * gelu_slope(pre_act), grad_product * activated], axis=1).astype(jnp.bfloat16)
        grad_in_proj = jnp.dot(normed_mlp.T, grad_expanded, preferred_element_type=jnp.float32)
        grad_normed_mlp = jnp.dot(grad_expanded, w_in.T, preferred_element_type=jnp.float32)
        grad_gain_two = lax.optimization_barrier(jnp.sum(grad_normed_mlp * normed_two, axis=0))
        grad_residual = grad_out.astype(jnp.float32) + norm_back(grad_normed_mlp * gain_second, normed_two, scale_two)
        residual_half = grad_residual.astype(jnp.bfloat16)
        grad_out_proj = jnp.dot(attended.T, residual_half, preferred_element_type=jnp.float32)
        grad_attended = jnp.dot(residual_half, w_out_attn.T, preferred_element_type=jnp.float32).astype(jnp.bfloat16)
        grad_att_heads = jnp.transpose(grad_attended.reshape(SEQ_TOK, HEADS, HD), (1, 0, 2))

        def head_backward(pieces):
            query_head, key_head, value_head, grad_head, attended_head, log_total = pieces
            scores = head_scores(query_head, key_head)
            probs = jnp.exp(scores - log_total)
            probs_half = probs.astype(jnp.bfloat16)
            grad_probs = jnp.dot(grad_head, value_head.T, preferred_element_type=jnp.float32)
            row_dots = lax.optimization_barrier(jnp.sum(grad_head.astype(jnp.float32) * attended_head.astype(jnp.float32), axis=-1, keepdims=True))
            grad_scores = (probs * (grad_probs - row_dots)).astype(jnp.bfloat16)
            grad_query = jnp.dot(grad_scores, key_head, preferred_element_type=jnp.float32) * scale
            grad_key = jnp.dot(grad_scores.T, query_head, preferred_element_type=jnp.float32) * scale
            grad_value = jnp.dot(probs_half.T, grad_head, preferred_element_type=jnp.float32)
            return (grad_query, grad_key, grad_value)
        grad_q_heads, grad_k_heads, grad_v_heads = lax.map(head_backward, (query_heads, key_heads, value_heads, grad_att_heads, attended_heads, log_totals))
        grad_queries = unrotate(jnp.transpose(grad_q_heads, (1, 0, 2)), cosine, sine).reshape(SEQ_TOK, D)
        grad_keys = unrotate(jnp.transpose(grad_k_heads, (1, 0, 2)), cosine, sine).reshape(SEQ_TOK, D)
        grad_values = jnp.transpose(grad_v_heads, (1, 0, 2)).reshape(SEQ_TOK, D)
        grad_projected = jnp.concatenate([grad_queries, grad_keys, grad_values], axis=1).astype(jnp.bfloat16)
        grad_qkv = jnp.dot(normed_attn.T, grad_projected, preferred_element_type=jnp.float32)
        grad_normed_attn = jnp.dot(grad_projected, w_qkv.T, preferred_element_type=jnp.float32)
        grad_gain_one = lax.optimization_barrier(jnp.sum(grad_normed_attn * normed_one, axis=0))
        grad_tokens = (grad_residual + norm_back(grad_normed_attn * gain_first, normed_one, scale_one)).astype(jnp.bfloat16)
        totals = (carry[0] + grad_qkv, carry[1] + grad_out_proj, carry[2] + grad_in_proj, carry[3] + grad_mlp_out, carry[4] + grad_gain_one, carry[5] + grad_gain_two)
        return (totals, (block_out, grad_tokens))
    zeros = (jnp.zeros((D, 3 * D), jnp.float32), jnp.zeros((D, D), jnp.float32), jnp.zeros((D, 2 * FF), jnp.float32), jnp.zeros((FF, D), jnp.float32), jnp.zeros((D,), jnp.float32), jnp.zeros((D,), jnp.float32))
    totals, stacked = lax.scan(one_row, zeros, (inputs, segment_ids, cotangent))
    return (stacked[0], stacked[1], totals[0], totals[1], totals[2], totals[3], totals[4], totals[5])
```

```python
import math

import jax
import jax.numpy as jnp
from jax import lax
from jax.experimental import pallas as pl
from jax.experimental.pallas import tpu as pltpu
from jax.sharding import PartitionSpec as P

HEADS = 16
HD = 64


EPSILON = 1e-05
ROPE_BASE = 160000.0
MASKED = -1e30


def layer_norm(values):
    center = values - jnp.mean(values, axis=-1, keepdims=True)
    scaled = lax.rsqrt(jnp.mean(center * center, axis=-1, keepdims=True) + EPSILON)
    return (center * scaled, scaled)


def norm_back(grad_norm, normed, scaled):
    return scaled * (
        grad_norm
        - jnp.mean(grad_norm, axis=-1, keepdims=True)
        - normed * jnp.mean(grad_norm * normed, axis=-1, keepdims=True)
    )


def rope_columns(positions, head_size):
    freqs = ROPE_BASE ** (-jnp.arange(0, head_size, 2, dtype=jnp.float32) / head_size)
    angles = freqs[:, None] * positions[None, :]
    cosine = jnp.concatenate([jnp.cos(angles), jnp.cos(angles)], axis=0)
    sine = jnp.concatenate([jnp.sin(angles), jnp.sin(angles)], axis=0)
    return (cosine[None], sine[None])


def rotate_cols(values, cosine, sine):
    half = values.shape[1] // 2
    turned = jnp.concatenate([-values[:, half:], values[:, :half]], axis=1)
    return values * cosine + turned * sine


def unrotate_cols(grads, cosine, sine):
    half = grads.shape[1] // 2
    weighted = grads * sine
    turned = jnp.concatenate([weighted[:, half:], -weighted[:, :half]], axis=1)
    return grads * cosine + turned


def gelu_slope(values):
    return (
        0.5 * (1.0 + lax.erf(values * 0.7071067811865476))
        + values * jnp.exp(-0.5 * values * values) * 0.3989422804014327
    )


LANES = 128


def masked_scores(query, key, same, scale):
    scores = lax.dot_general(query, key, (((0,), (0,)), ((), ())), preferred_element_type=jnp.float32)
    return jnp.where(same, scores * scale, MASKED)


def same_segment(seg_own_ref, seg_ref, block):
    return seg_own_ref[...] == seg_ref[block, :, :]


def attend_kernel(scale, blocks, query_ref, key_ref, value_ref, seg_own_ref, seg_ref, out_ref, log_ref):
    query = query_ref[0]
    scores = [
        masked_scores(query, key_ref[b, 0, 0], same_segment(seg_own_ref, seg_ref, b), scale)
        for b in range(blocks)
    ]
    peak = scores[0]
    for b in range(1, blocks):
        peak = jnp.maximum(peak, scores[b])
    peak = jnp.max(peak, axis=-1, keepdims=True)
    total = jnp.exp(scores[0] - peak)
    for b in range(1, blocks):
        total = total + jnp.exp(scores[b] - peak)
    log_total = peak + jnp.log(jnp.sum(total, axis=-1, keepdims=True))
    log_ref[0] = log_total
    acc = None
    for b in range(blocks):
        probs = jnp.exp(scores[b] - log_total).astype(jnp.bfloat16)
        term = lax.dot_general(
            value_ref[b, 0, 0], probs, (((1,), (1,)), ((), ())), preferred_element_type=jnp.float32
        )
        acc = term if acc is None else acc + term
    out_ref[0] = acc.astype(jnp.bfloat16)


def attend_grad_kernel(
    scale,
    blocks,
    query_ref,
    key_ref,
    value_ref,
    seg_own_ref,
    seg_ref,
    log_ref,
    grad_ref,
    attended_ref,
    query_grad_ref,
    pair_ref,
):
    query = query_ref[0]
    grad = grad_ref[0]
    log_total = log_ref[0]
    dots_row = jnp.sum(
        grad.astype(jnp.float32) * attended_ref[0].astype(jnp.float32), axis=0, keepdims=True
    )
    dots = jnp.transpose(jnp.broadcast_to(dots_row, (8, dots_row.shape[1])))[:, :1]
    acc = None
    for b in range(blocks):
        key = key_ref[b, 0, 0]
        value = value_ref[b, 0, 0]
        scores = masked_scores(query, key, same_segment(seg_own_ref, seg_ref, b), scale)
        probs = jnp.exp(scores - log_total)
        grad_probs = lax.dot_general(
            grad, value, (((0,), (0,)), ((), ())), preferred_element_type=jnp.float32
        )
        grad_scores = (probs * (grad_probs - dots)).astype(jnp.bfloat16)
        term = lax.dot_general(
            key, grad_scores, (((1,), (1,)), ((), ())), preferred_element_type=jnp.float32
        )
        acc = term if acc is None else acc + term
        key_grad = lax.dot_general(
            query, grad_scores, (((1,), (0,)), ((), ())), preferred_element_type=jnp.float32
        )
        value_grad = lax.dot_general(
            grad,
            probs.astype(jnp.bfloat16),
            (((1,), (0,)), ((), ())),
            preferred_element_type=jnp.float32,
        )
        pair_ref[b, 0, 0] = (key_grad * scale).astype(jnp.bfloat16)
        pair_ref[b, 1, 0] = value_grad.astype(jnp.bfloat16)
    query_grad_ref[0] = acc * scale


def attention_specs(blocks, head_size, tok_count):
    head = pl.BlockSpec((1, head_size, tok_count), lambda h: (h, 0, 0))
    keys = pl.BlockSpec((blocks, 1, 1, head_size, tok_count), lambda h: (0, 0, h, 0, 0))
    values = pl.BlockSpec((blocks, 1, 1, head_size, tok_count), lambda h: (0, 1, h, 0, 0))
    pairs = pl.BlockSpec((blocks, 2, 1, head_size, tok_count), lambda h: (0, 0, h, 0, 0))
    seg_own = pl.BlockSpec((tok_count, 1), lambda h: (0, 0))
    seg_all = pl.BlockSpec((blocks, 1, tok_count), lambda h: (0, 0, 0))
    log = pl.BlockSpec((1, tok_count, 1), lambda h: (h, 0, 0))
    return head, keys, values, pairs, seg_own, seg_all, log


def attend(query_cols, pairs_all, seg_own, seg_all, scale):
    heads, head_size, tok_count = query_cols.shape
    blocks = pairs_all.shape[0]
    head, keys, values, pairs, own, every, log = attention_specs(blocks, head_size, tok_count)
    return pl.pallas_call(
        lambda *refs: attend_kernel(scale, blocks, *refs),
        grid=(heads,),
        in_specs=[head, keys, values, own, every],
        out_specs=[head, log],
        out_shape=[
            jax.ShapeDtypeStruct((heads, head_size, tok_count), jnp.bfloat16),
            jax.ShapeDtypeStruct((heads, tok_count, 1), jnp.float32),
        ],
        name="attend",
    )(query_cols, pairs_all, pairs_all, seg_own, seg_all)


def attend_grads(query_cols, pairs_all, seg_own, seg_all, log_total, grad_cols, attended_cols, scale):
    heads, head_size, tok_count = query_cols.shape
    blocks = pairs_all.shape[0]
    head, keys, values, pairs, own, every, log = attention_specs(blocks, head_size, tok_count)
    return pl.pallas_call(
        lambda *refs: attend_grad_kernel(scale, blocks, *refs),
        grid=(heads,),
        in_specs=[head, keys, values, own, every, log, head, head],
        out_specs=[head, pairs],
        out_shape=[
            jax.ShapeDtypeStruct((heads, head_size, tok_count), jnp.float32),
            jax.ShapeDtypeStruct((blocks, 2, heads, head_size, tok_count), jnp.bfloat16),
        ],
        name="attend_grads",
    )(query_cols, pairs_all, pairs_all, seg_own, seg_all, log_total, grad_cols, attended_cols)


def body(inputs, segment_ids, gain_attn, w_qkv, w_out_attn, gain_mlp, w_in, w_out_mlp, cotangent):
    tokens = inputs[0].astype(jnp.float32)
    tok_count, width = tokens.shape
    heads = HEADS
    head_size = HD
    scale = 1.0 / math.sqrt(head_size)
    everyone = ("ctx", "fsdp")
    hidden_units = w_out_mlp.shape[0]
    gains_own = jnp.concatenate(
        [
            gain_attn[:, None],
            gain_mlp[:, None],
            jnp.zeros((gain_attn.shape[0], LANES - 2), jnp.bfloat16),
        ],
        axis=1,
    )
    first_full = lax.all_gather(
        jnp.concatenate([w_qkv, gains_own], axis=1), everyone, axis=0, tiled=True
    )
    rest_own = jnp.concatenate([w_out_attn, w_in, w_out_mlp.T], axis=1)
    qkv_full = first_full[:, : 3 * width]
    gains = first_full[:, 3 * width : 3 * width + 2].astype(jnp.float32).T
    gain_first = gains[0]
    gain_second = gains[1]
    normed_one, scale_one = layer_norm(tokens)
    normed_attn = (normed_one * gain_first).astype(jnp.bfloat16)
    projected_cols = jnp.einsum(
        "de,td->et", qkv_full, normed_attn, preferred_element_type=jnp.float32
    )
    positions = (lax.axis_index("ctx") * tok_count + jnp.arange(tok_count, dtype=jnp.int32)).astype(
        jnp.float32
    )
    cosine, sine = rope_columns(positions, head_size)
    query_cols = rotate_cols(
        projected_cols[:width].reshape(heads, head_size, tok_count), cosine, sine
    ).astype(jnp.bfloat16)
    key_cols = rotate_cols(
        projected_cols[width : 2 * width].reshape(heads, head_size, tok_count), cosine, sine
    ).astype(jnp.bfloat16)
    value_cols = projected_cols[2 * width :].astype(jnp.bfloat16)
    seg_row = segment_ids.astype(jnp.bfloat16)
    packed = lax.all_gather(
        jnp.concatenate(
            [
                key_cols.reshape(width, tok_count),
                value_cols,
                jnp.broadcast_to(seg_row, (16, tok_count)),
            ],
            axis=0,
        ),
        "ctx",
        axis=0,
        tiled=True,
    )
    blocks = packed.shape[0] // (2 * width + 16)
    packed = packed.reshape(blocks, 2 * width + 16, tok_count)
    rest_full = lax.all_gather(rest_own, everyone, axis=0, tiled=True)
    attn_full = rest_full[:, :width]
    in_full = rest_full[:, width : width + 2 * hidden_units]
    mlp_turned = rest_full[:, width + 2 * hidden_units :]
    pairs_all = packed[:, : 2 * width].reshape(blocks, 2, heads, head_size, tok_count)
    seg_all = packed[:, 2 * width : 2 * width + 1].astype(jnp.float32)
    seg_own = segment_ids.astype(jnp.float32).T
    attended_cols, log_total = attend(query_cols, pairs_all, seg_own, seg_all, scale)
    attended = attended_cols.reshape(width, tok_count).T
    residual = tokens + jnp.dot(attended, attn_full, preferred_element_type=jnp.float32)
    normed_two, scale_two = layer_norm(residual)
    normed_mlp = (normed_two * gain_second).astype(jnp.bfloat16)
    expanded = jnp.dot(normed_mlp, in_full, preferred_element_type=jnp.float32)
    pre_act = expanded[:, :hidden_units]
    gate_part = expanded[:, hidden_units:]
    activated = jax.nn.gelu(pre_act, approximate=False)
    product = (activated * gate_part).astype(jnp.bfloat16)
    block_out = (
        residual
        + jnp.einsum("tf,df->td", product, mlp_turned, preferred_element_type=jnp.float32)
    ).astype(jnp.bfloat16)
    grad_out = cotangent[0]
    grad_product = jnp.einsum("td,df->tf", grad_out, mlp_turned, preferred_element_type=jnp.float32)
    grad_expanded = jnp.concatenate(
        [grad_product * gate_part * gelu_slope(pre_act), grad_product * activated], axis=1
    ).astype(jnp.bfloat16)
    grad_normed_mlp = jnp.einsum(
        "tf,df->td", grad_expanded, in_full, preferred_element_type=jnp.float32
    )
    grad_gain_two = jnp.sum(grad_normed_mlp * normed_two, axis=0)
    mlp_rows = lax.psum_scatter(
        jnp.concatenate(
            [
                jnp.einsum(
                    "td,tf->df", normed_mlp, grad_expanded, preferred_element_type=jnp.float32
                ).astype(jnp.bfloat16),
                jnp.einsum(
                    "td,tf->df", grad_out, product, preferred_element_type=jnp.float32
                ).astype(jnp.bfloat16),
            ],
            axis=1,
        ),
        everyone,
        scatter_dimension=0,
        tiled=True,
    )
    grad_residual = grad_out.astype(jnp.float32) + norm_back(
        grad_normed_mlp * gain_second, normed_two, scale_two
    )
    residual_half = grad_residual.astype(jnp.bfloat16)
    grad_attended = jnp.einsum(
        "te,de->dt", residual_half, attn_full, preferred_element_type=jnp.float32
    ).astype(jnp.bfloat16)
    grad_att_cols = grad_attended.reshape(heads, head_size, tok_count)
    grad_query_cols, pair_parts = attend_grads(
        query_cols, pairs_all, seg_own, seg_all, log_total, grad_att_cols, attended_cols, scale
    )
    pair_sums = lax.psum_scatter(
        pair_parts.reshape(blocks * 2 * width, tok_count), "ctx", scatter_dimension=0, tiled=True
    )
    grad_keys = pair_sums[:width].astype(jnp.float32)
    grad_values = pair_sums[width:]
    grad_key_cols = grad_keys.reshape(heads, head_size, tok_count)
    grad_query_rot = unrotate_cols(grad_query_cols, cosine, sine).reshape(width, tok_count)
    grad_key_rot = unrotate_cols(grad_key_cols, cosine, sine).reshape(width, tok_count)
    grad_proj_cols = jnp.concatenate(
        [grad_query_rot.astype(jnp.bfloat16), grad_key_rot.astype(jnp.bfloat16), grad_values], axis=0
    )
    grad_normed_attn = jnp.einsum(
        "de,et->td", qkv_full, grad_proj_cols, preferred_element_type=jnp.float32
    )
    grad_gain_one = jnp.sum(grad_normed_attn * normed_one, axis=0)
    gain_cols = jnp.concatenate(
        [
            jnp.stack([grad_gain_one, grad_gain_two], axis=0),
            jnp.zeros((LANES - 2, width), jnp.float32),
        ],
        axis=0,
    ).T.astype(jnp.bfloat16)
    attn_rows = lax.psum_scatter(
        jnp.concatenate(
            [
                jnp.einsum(
                    "td,et->de", normed_attn, grad_proj_cols, preferred_element_type=jnp.float32
                ).astype(jnp.bfloat16),
                jnp.einsum(
                    "td,te->de", attended, residual_half, preferred_element_type=jnp.float32
                ).astype(jnp.bfloat16),
                gain_cols,
            ],
            axis=1,
        ),
        everyone,
        scatter_dimension=0,
        tiled=True,
    )
    grad_tokens = (
        grad_residual + norm_back(grad_normed_attn * gain_first, normed_one, scale_one)
    ).astype(jnp.bfloat16)
    attn_sums = attn_rows.astype(jnp.float32)
    mlp_sums = mlp_rows.astype(jnp.float32)
    grad_qkv_rows = attn_sums[:, : 3 * width]
    grad_attn_rows = attn_sums[:, 3 * width : 4 * width]
    gain_sum_one = attn_sums[:, 4 * width]
    gain_sum_two = attn_sums[:, 4 * width + 1]
    grad_in_rows = mlp_sums[:, : 2 * hidden_units]
    grad_mlp_cols = mlp_sums[:, 2 * hidden_units :].T
    return (
        block_out[None],
        grad_tokens[None],
        grad_qkv_rows,
        grad_attn_rows,
        grad_in_rows,
        grad_mlp_cols,
        gain_sum_one,
        gain_sum_two,
    )


def solution(mesh):
    in_specs = (
        P("fsdp", "ctx", None),
        P("fsdp", "ctx"),
        P(("ctx", "fsdp")),
        P(("ctx", "fsdp"), None),
        P(("ctx", "fsdp"), None),
        P(("ctx", "fsdp")),
        P(("ctx", "fsdp"), None),
        P(None, ("ctx", "fsdp")),
        P("fsdp", "ctx", None),
    )
    out_specs = (
        P("fsdp", "ctx", None),
        P("fsdp", "ctx", None),
        P(("ctx", "fsdp"), None),
        P(("ctx", "fsdp"), None),
        P(("ctx", "fsdp"), None),
        P(None, ("ctx", "fsdp")),
        P(("ctx", "fsdp")),
        P(("ctx", "fsdp")),
    )
    return jax.shard_map(body, mesh=mesh, in_specs=in_specs, out_specs=out_specs, check_vma=False)
```

```python
import functools
import math

import jax
import jax.numpy as jnp
from jax import lax
from jax.experimental import pallas as pl
from jax.experimental.pallas import tpu as pltpu
from jax.sharding import PartitionSpec as P

HEADS = 16
HD = 64


EPSILON = 1e-05
ROPE_BASE = 160000.0
MASKED = -1e30


def layer_norm(values):
    center = values - jnp.mean(values, axis=-1, keepdims=True)
    scaled = lax.rsqrt(jnp.mean(center * center, axis=-1, keepdims=True) + EPSILON)
    return (center * scaled, scaled)


def norm_back(grad_norm, normed, scaled):
    return scaled * (
        grad_norm
        - jnp.mean(grad_norm, axis=-1, keepdims=True)
        - normed * jnp.mean(grad_norm * normed, axis=-1, keepdims=True)
    )


def rope_columns(positions, head_size):
    freqs = ROPE_BASE ** (-jnp.arange(0, head_size, 2, dtype=jnp.float32) / head_size)
    angles = freqs[:, None] * positions[None, :]
    cosine = jnp.concatenate([jnp.cos(angles), jnp.cos(angles)], axis=0)
    sine = jnp.concatenate([jnp.sin(angles), jnp.sin(angles)], axis=0)
    return (cosine[None], sine[None])


def rotate_cols(values, cosine, sine):
    half = values.shape[1] // 2
    turned = jnp.concatenate([-values[:, half:], values[:, :half]], axis=1)
    return values * cosine + turned * sine


def unrotate_cols(grads, cosine, sine):
    half = grads.shape[1] // 2
    weighted = grads * sine
    turned = jnp.concatenate([weighted[:, half:], -weighted[:, :half]], axis=1)
    return grads * cosine + turned


def gelu_slope(values):
    return (
        0.5 * (1.0 + lax.erf(values * 0.7071067811865476))
        + values * jnp.exp(-0.5 * values * values) * 0.3989422804014327
    )


LANES = 128
SEG_ROWS = 16
QUERY_BLOCK = 256


def masked_scores(query, key, same, scale):
    scores = lax.dot_general(query, key, (((0,), (0,)), ((), ())), preferred_element_type=jnp.float32)
    return jnp.where(same, scores * scale, MASKED)


def attend_kernel(scale, query_ref, key_ref, value_ref, seg_own_ref, seg_ref, out_ref, log_ref):
    same = seg_own_ref[...] == seg_ref[...]
    scores = masked_scores(query_ref[0], key_ref[0], same, scale)
    peak = jnp.max(scores, axis=-1, keepdims=True)
    log_total = peak + jnp.log(jnp.sum(jnp.exp(scores - peak), axis=-1, keepdims=True))
    log_ref[0] = log_total
    probs = jnp.exp(scores - log_total).astype(jnp.bfloat16)
    out_ref[0] = lax.dot_general(
        value_ref[0], probs, (((1,), (1,)), ((), ())), preferred_element_type=jnp.float32
    ).astype(jnp.bfloat16)


def attend_grad_kernel(
    scale,
    query_ref,
    key_ref,
    value_ref,
    seg_own_ref,
    seg_ref,
    log_ref,
    grad_ref,
    attended_ref,
    query_grad_ref,
    key_grad_ref,
    value_grad_ref,
):
    @pl.when(pl.program_id(1) == 0)
    def _():
        key_grad_ref[...] = jnp.zeros_like(key_grad_ref)
        value_grad_ref[...] = jnp.zeros_like(value_grad_ref)

    query = query_ref[0]
    grad = grad_ref[0]
    key = key_ref[0]
    dots_row = jnp.sum(
        grad.astype(jnp.float32) * attended_ref[0].astype(jnp.float32), axis=0, keepdims=True
    )
    dots = jnp.transpose(jnp.broadcast_to(dots_row, (8, dots_row.shape[1])))[:, :1]
    same = seg_own_ref[...] == seg_ref[...]
    probs = jnp.exp(masked_scores(query, key, same, scale) - log_ref[0])
    grad_probs = lax.dot_general(
        grad, value_ref[0], (((0,), (0,)), ((), ())), preferred_element_type=jnp.float32
    )
    grad_scores = (probs * (grad_probs - dots)).astype(jnp.bfloat16)
    query_grad_ref[0] = scale * lax.dot_general(
        key, grad_scores, (((1,), (1,)), ((), ())), preferred_element_type=jnp.float32
    )
    key_grad_ref[0] += scale * lax.dot_general(
        query, grad_scores, (((1,), (0,)), ((), ())), preferred_element_type=jnp.float32
    )
    value_grad_ref[0] += lax.dot_general(
        grad, probs.astype(jnp.bfloat16), (((1,), (0,)), ((), ())), preferred_element_type=jnp.float32
    )


def attention_specs(head_size, row_count, block):
    part = pl.BlockSpec((1, head_size, block), lambda h, b: (h, 0, b))
    full = pl.BlockSpec((1, head_size, row_count), lambda h, b: (h, 0, 0))
    seg_own = pl.BlockSpec((block, 1), lambda h, b: (b, 0))
    seg_all = pl.BlockSpec((1, row_count), lambda h, b: (0, 0))
    log = pl.BlockSpec((1, block, 1), lambda h, b: (h, b, 0))
    return part, full, seg_own, seg_all, log


def attend(query_cols, key_cols, value_cols, seg_col, seg_row, scale):
    heads, head_size, row_count = query_cols.shape
    block = min(QUERY_BLOCK, row_count)
    part, full, own, every, log = attention_specs(head_size, row_count, block)
    return pl.pallas_call(
        lambda *refs: attend_kernel(scale, *refs),
        grid=(heads, row_count // block),
        in_specs=[part, full, full, own, every],
        out_specs=[part, log],
        out_shape=[
            jax.ShapeDtypeStruct((heads, head_size, row_count), jnp.bfloat16),
            jax.ShapeDtypeStruct((heads, row_count, 1), jnp.float32),
        ],
        name="attend",
    )(query_cols, key_cols, value_cols, seg_col, seg_row)


def attend_grads(
    query_cols, key_cols, value_cols, seg_col, seg_row, log_total, grad_cols, attended_cols, scale
):
    heads, head_size, row_count = query_cols.shape
    block = min(QUERY_BLOCK, row_count)
    part, full, own, every, log = attention_specs(head_size, row_count, block)
    grads = jax.ShapeDtypeStruct((heads, head_size, row_count), jnp.float32)
    return pl.pallas_call(
        lambda *refs: attend_grad_kernel(scale, *refs),
        grid=(heads, row_count // block),
        in_specs=[part, full, full, own, every, log, part, part],
        out_specs=[part, full, full],
        out_shape=[grads, grads, grads],
        name="attend_grads",
    )(query_cols, key_cols, value_cols, seg_col, seg_row, log_total, grad_cols, attended_cols)


def body(
    ctx_size,
    fsdp_size,
    inputs,
    segment_ids,
    gain_attn,
    w_qkv,
    w_out_attn,
    gain_mlp,
    w_in,
    w_out_mlp,
    cotangent,
):
    tok_count, width = inputs.shape[1:]
    heads = HEADS
    head_size = HD
    scale = 1.0 / math.sqrt(head_size)
    everyone = ("ctx", "fsdp")
    hidden_units = w_out_mlp.shape[0]
    row_count = ctx_size * tok_count
    devices = ctx_size * fsdp_size
    own_heads = heads // ctx_size
    own_width = own_heads * head_size
    weight_rows = w_qkv.shape[0]

    seg_block = jnp.pad(segment_ids.astype(jnp.bfloat16), ((0, SEG_ROWS - 1), (0, width - tok_count)))
    gathered = lax.all_gather(
        jnp.concatenate([inputs[0], seg_block], axis=0), "ctx", axis=0, tiled=True
    ).reshape(ctx_size, tok_count + SEG_ROWS, width)

    qkv_parts = jnp.transpose(
        w_qkv.reshape(weight_rows, 3, ctx_size, own_width), (2, 0, 1, 3)
    ).reshape(ctx_size, weight_rows, 3 * own_width)
    gains_own = jnp.pad(jnp.stack([gain_attn, gain_mlp], axis=1), ((0, 0), (0, LANES - 2)))
    qkv_parts = jnp.concatenate(
        [qkv_parts, jnp.broadcast_to(gains_own, (ctx_size, weight_rows, LANES))], axis=2
    )
    qkv_parts = jnp.broadcast_to(
        qkv_parts[:, None], (ctx_size, fsdp_size, weight_rows, 3 * own_width + LANES)
    ).reshape(devices, weight_rows, 3 * own_width + LANES)
    qkv_got = lax.all_to_all(qkv_parts, everyone, 0, 0, tiled=True).reshape(
        devices * weight_rows, 3 * own_width + LANES
    )
    qkv_mine = qkv_got[:, : 3 * own_width]
    gains = qkv_got[:, 3 * own_width : 3 * own_width + 2].astype(jnp.float32).T
    gain_first = gains[0]
    gain_second = gains[1]

    rest_own = jnp.concatenate([w_out_attn, w_in, w_out_mlp.T], axis=1)
    rest_own, gathered = lax.optimization_barrier((rest_own, gathered))
    rest_full = lax.all_gather(rest_own, everyone, axis=0, tiled=True)
    attn_full = rest_full[:, :width]
    in_full = rest_full[:, width : width + 2 * hidden_units]
    mlp_turned = rest_full[:, width + 2 * hidden_units :]

    seg_row = gathered[:, tok_count, :tok_count].reshape(1, row_count).astype(jnp.float32)
    seg_col = seg_row.reshape(row_count, 1)
    row_tokens = gathered[:, :tok_count].reshape(row_count, width).astype(jnp.float32)
    row_normed, unused = layer_norm(row_tokens)
    row_normed_attn = (row_normed * gain_first).astype(jnp.bfloat16)
    tokens = inputs[0].astype(jnp.float32)
    normed_one, scale_one = layer_norm(tokens)

    projected_cols = jnp.einsum(
        "de,td->et", qkv_mine, row_normed_attn, preferred_element_type=jnp.float32
    ).reshape(3, own_heads, head_size, row_count)
    positions = jnp.arange(row_count, dtype=jnp.int32).astype(jnp.float32)
    cosine, sine = rope_columns(positions, head_size)
    query_cols = rotate_cols(projected_cols[0], cosine, sine).astype(jnp.bfloat16)
    key_cols = rotate_cols(projected_cols[1], cosine, sine).astype(jnp.bfloat16)
    value_cols = projected_cols[2].astype(jnp.bfloat16)
    row_attended, log_total = attend(query_cols, key_cols, value_cols, seg_col, seg_row, scale)

    attended = lax.all_to_all(
        row_attended.reshape(own_width, row_count).T.reshape(ctx_size, tok_count, own_width),
        "ctx",
        0,
        0,
        tiled=True,
    )
    attended = jnp.transpose(attended, (1, 0, 2)).reshape(tok_count, width)
    residual = tokens + jnp.dot(attended, attn_full, preferred_element_type=jnp.float32)
    normed_two, scale_two = layer_norm(residual)
    normed_mlp = (normed_two * gain_second).astype(jnp.bfloat16)
    expanded = jnp.dot(normed_mlp, in_full, preferred_element_type=jnp.float32)
    pre_act = expanded[:, :hidden_units]
    gate_part = expanded[:, hidden_units:]
    activated = jax.nn.gelu(pre_act, approximate=False)
    product = (activated * gate_part).astype(jnp.bfloat16)
    block_out = (
        residual
        + jnp.einsum("tf,df->td", product, mlp_turned, preferred_element_type=jnp.float32)
    ).astype(jnp.bfloat16)
    grad_out = cotangent[0]
    grad_product = jnp.einsum("td,df->tf", grad_out, mlp_turned, preferred_element_type=jnp.float32)
    grad_expanded = jnp.concatenate(
        [grad_product * gate_part * gelu_slope(pre_act), grad_product * activated], axis=1
    ).astype(jnp.bfloat16)
    grad_normed_mlp = jnp.einsum(
        "tf,df->td", grad_expanded, in_full, preferred_element_type=jnp.float32
    )
    grad_gain_two = jnp.sum(grad_normed_mlp * normed_two, axis=0)
    grad_residual = grad_out.astype(jnp.float32) + norm_back(
        grad_normed_mlp * gain_second, normed_two, scale_two
    )
    residual_half = grad_residual.astype(jnp.bfloat16)
    gain_block = jnp.pad(grad_gain_two[:, None], ((0, 0), (0, LANES - 1))).astype(jnp.bfloat16)
    weight_sums = lax.psum_scatter(
        jnp.concatenate(
            [
                jnp.einsum(
                    "td,te->de", attended, residual_half, preferred_element_type=jnp.float32
                ).astype(jnp.bfloat16),
                jnp.einsum(
                    "td,tf->df", normed_mlp, grad_expanded, preferred_element_type=jnp.float32
                ).astype(jnp.bfloat16),
                jnp.einsum(
                    "td,tf->df", grad_out, product, preferred_element_type=jnp.float32
                ).astype(jnp.bfloat16),
                gain_block,
            ],
            axis=1,
        ),
        everyone,
        scatter_dimension=0,
        tiled=True,
    ).astype(jnp.float32)
    grad_attended = jnp.einsum(
        "te,de->td", residual_half, attn_full, preferred_element_type=jnp.float32
    ).astype(jnp.bfloat16)
    row_grad = lax.all_to_all(
        jnp.transpose(grad_attended.reshape(tok_count, ctx_size, own_width), (1, 0, 2)),
        "ctx",
        0,
        0,
        tiled=True,
    )
    row_grad_cols = row_grad.reshape(row_count, own_width).T.reshape(
        own_heads, head_size, row_count
    )
    grad_query, grad_key, grad_value = attend_grads(
        query_cols,
        key_cols,
        value_cols,
        seg_col,
        seg_row,
        log_total,
        row_grad_cols,
        row_attended,
        scale,
    )
    grad_proj_cols = (
        jnp.stack(
            [
                unrotate_cols(grad_query, cosine, sine),
                unrotate_cols(grad_key, cosine, sine),
                grad_value,
            ],
            axis=0,
        )
        .astype(jnp.bfloat16)
        .reshape(3 * own_width, row_count)
    )
    row_grad_normed = jnp.einsum(
        "de,et->td", qkv_mine, grad_proj_cols, preferred_element_type=jnp.float32
    )
    grad_gain_part = jnp.sum(row_grad_normed * row_normed, axis=0)
    grad_normed_attn = jnp.sum(
        lax.all_to_all(
            row_grad_normed.astype(jnp.bfloat16).reshape(ctx_size, tok_count, width),
            "ctx",
            0,
            0,
            tiled=True,
        ).astype(jnp.float32),
        axis=0,
    )
    qkv_terms = jnp.concatenate(
        [
            jnp.einsum(
                "td,et->de", row_normed_attn, grad_proj_cols, preferred_element_type=jnp.float32
            ).astype(jnp.bfloat16),
            jnp.pad(grad_gain_part[:, None], ((0, 0), (0, LANES - 1))).astype(jnp.bfloat16),
        ],
        axis=1,
    ).reshape(devices, weight_rows, 3 * own_width + LANES)
    qkv_sums = jnp.sum(
        lax.all_to_all(qkv_terms, everyone, 0, 0, tiled=True)
        .reshape(ctx_size, fsdp_size, weight_rows, 3 * own_width + LANES)
        .astype(jnp.float32),
        axis=1,
    )
    grad_qkv_rows = jnp.transpose(
        qkv_sums[:, :, : 3 * own_width].reshape(ctx_size, weight_rows, 3, own_width), (1, 2, 0, 3)
    ).reshape(weight_rows, 3 * width)
    gain_sum_one = jnp.sum(qkv_sums[:, :, 3 * own_width], axis=0)
    grad_tokens = (
        grad_residual + norm_back(grad_normed_attn * gain_first, normed_one, scale_one)
    ).astype(jnp.bfloat16)
    grad_attn_rows = weight_sums[:, :width]
    grad_in_rows = weight_sums[:, width : width + 2 * hidden_units]
    grad_mlp_cols = weight_sums[:, width + 2 * hidden_units : width + 3 * hidden_units].T
    gain_sum_two = weight_sums[:, width + 3 * hidden_units]
    return (
        block_out[None],
        grad_tokens[None],
        grad_qkv_rows,
        grad_attn_rows,
        grad_in_rows,
        grad_mlp_cols,
        gain_sum_one,
        gain_sum_two,
    )


def solution(mesh):
    in_specs = (
        P("fsdp", "ctx", None),
        P("fsdp", "ctx"),
        P(("ctx", "fsdp")),
        P(("ctx", "fsdp"), None),
        P(("ctx", "fsdp"), None),
        P(("ctx", "fsdp")),
        P(("ctx", "fsdp"), None),
        P(None, ("ctx", "fsdp")),
        P("fsdp", "ctx", None),
    )
    out_specs = (
        P("fsdp", "ctx", None),
        P("fsdp", "ctx", None),
        P(("ctx", "fsdp"), None),
        P(("ctx", "fsdp"), None),
        P(("ctx", "fsdp"), None),
        P(None, ("ctx", "fsdp")),
        P(("ctx", "fsdp")),
        P(("ctx", "fsdp")),
    )
    step = functools.partial(body, mesh.shape["ctx"], mesh.shape["fsdp"])
    return jax.shard_map(step, mesh=mesh, in_specs=in_specs, out_specs=out_specs, check_vma=False)
```

```python
import functools
import math

import jax
import jax.numpy as jnp
from jax import lax
from jax.experimental import pallas as pl
from jax.experimental.pallas import tpu as pltpu
from jax.sharding import PartitionSpec as P

HEADS = 16
HD = 64


EPSILON = 1e-05
ROPE_BASE = 160000.0
MASKED = -1e30


def layer_norm(values):
    center = values - jnp.mean(values, axis=-1, keepdims=True)
    scaled = lax.rsqrt(jnp.mean(center * center, axis=-1, keepdims=True) + EPSILON)
    return (center * scaled, scaled)


def norm_back(grad_norm, normed, scaled):
    return scaled * (
        grad_norm
        - jnp.mean(grad_norm, axis=-1, keepdims=True)
        - normed * jnp.mean(grad_norm * normed, axis=-1, keepdims=True)
    )


def rope_columns(positions, head_size):
    freqs = ROPE_BASE ** (-jnp.arange(0, head_size, 2, dtype=jnp.float32) / head_size)
    angles = freqs[:, None] * positions[None, :]
    cosine = jnp.concatenate([jnp.cos(angles), jnp.cos(angles)], axis=0)
    sine = jnp.concatenate([jnp.sin(angles), jnp.sin(angles)], axis=0)
    return (cosine[None], sine[None])


def rotate_cols(values, cosine, sine):
    half = values.shape[1] // 2
    turned = jnp.concatenate([-values[:, half:], values[:, :half]], axis=1)
    return values * cosine + turned * sine


def unrotate_cols(grads, cosine, sine):
    half = grads.shape[1] // 2
    weighted = grads * sine
    turned = jnp.concatenate([weighted[:, half:], -weighted[:, :half]], axis=1)
    return grads * cosine + turned


def gelu_slope(values):
    return (
        0.5 * (1.0 + lax.erf(values * 0.7071067811865476))
        + values * jnp.exp(-0.5 * values * values) * 0.3989422804014327
    )


LANES = 128
SEG_ROWS = 16
QUERY_BLOCK = 256


def masked_scores(query, key, same, scale):
    scores = lax.dot_general(query, key, (((0,), (0,)), ((), ())), preferred_element_type=jnp.float32)
    return jnp.where(same, scores * scale, MASKED)


def attend_kernel(scale, query_ref, key_ref, value_ref, seg_own_ref, seg_ref, out_ref, log_ref):
    same = seg_own_ref[...] == seg_ref[...]
    scores = masked_scores(query_ref[0], key_ref[0], same, scale)
    peak = jnp.max(scores, axis=-1, keepdims=True)
    log_total = peak + jnp.log(jnp.sum(jnp.exp(scores - peak), axis=-1, keepdims=True))
    log_ref[0] = log_total
    probs = jnp.exp(scores - log_total).astype(jnp.bfloat16)
    out_ref[0] = lax.dot_general(
        value_ref[0], probs, (((1,), (1,)), ((), ())), preferred_element_type=jnp.float32
    ).astype(jnp.bfloat16)


def attend_grad_kernel(
    scale,
    query_ref,
    key_ref,
    value_ref,
    seg_own_ref,
    seg_ref,
    log_ref,
    grad_ref,
    attended_ref,
    query_grad_ref,
    key_grad_ref,
    value_grad_ref,
):
    @pl.when(pl.program_id(1) == 0)
    def _():
        key_grad_ref[...] = jnp.zeros_like(key_grad_ref)
        value_grad_ref[...] = jnp.zeros_like(value_grad_ref)

    query = query_ref[0]
    grad = grad_ref[0]
    key = key_ref[0]
    dots_row = jnp.sum(
        grad.astype(jnp.float32) * attended_ref[0].astype(jnp.float32), axis=0, keepdims=True
    )
    dots = jnp.transpose(jnp.broadcast_to(dots_row, (8, dots_row.shape[1])))[:, :1]
    same = seg_own_ref[...] == seg_ref[...]
    probs = jnp.exp(masked_scores(query, key, same, scale) - log_ref[0])
    grad_probs = lax.dot_general(
        grad, value_ref[0], (((0,), (0,)), ((), ())), preferred_element_type=jnp.float32
    )
    grad_scores = (probs * (grad_probs - dots)).astype(jnp.bfloat16)
    query_grad_ref[0] = scale * lax.dot_general(
        key, grad_scores, (((1,), (1,)), ((), ())), preferred_element_type=jnp.float32
    )
    key_grad_ref[0] += scale * lax.dot_general(
        query, grad_scores, (((1,), (0,)), ((), ())), preferred_element_type=jnp.float32
    )
    value_grad_ref[0] += lax.dot_general(
        grad, probs.astype(jnp.bfloat16), (((1,), (0,)), ((), ())), preferred_element_type=jnp.float32
    )


def attention_specs(head_size, row_count, block):
    part = pl.BlockSpec((1, head_size, block), lambda h, b: (h, 0, b))
    full = pl.BlockSpec((1, head_size, row_count), lambda h, b: (h, 0, 0))
    seg_own = pl.BlockSpec((block, 1), lambda h, b: (b, 0))
    seg_all = pl.BlockSpec((1, row_count), lambda h, b: (0, 0))
    log = pl.BlockSpec((1, block, 1), lambda h, b: (h, b, 0))
    return part, full, seg_own, seg_all, log


def attend(query_cols, key_cols, value_cols, seg_col, seg_row, scale):
    heads, head_size, row_count = query_cols.shape
    block = min(QUERY_BLOCK, row_count)
    part, full, own, every, log = attention_specs(head_size, row_count, block)
    return pl.pallas_call(
        lambda *refs: attend_kernel(scale, *refs),
        grid=(heads, row_count // block),
        in_specs=[part, full, full, own, every],
        out_specs=[part, log],
        out_shape=[
            jax.ShapeDtypeStruct((heads, head_size, row_count), jnp.bfloat16),
            jax.ShapeDtypeStruct((heads, row_count, 1), jnp.float32),
        ],
        name="attend",
    )(query_cols, key_cols, value_cols, seg_col, seg_row)


def attend_grads(
    query_cols, key_cols, value_cols, seg_col, seg_row, log_total, grad_cols, attended_cols, scale
):
    heads, head_size, row_count = query_cols.shape
    block = min(QUERY_BLOCK, row_count)
    part, full, own, every, log = attention_specs(head_size, row_count, block)
    grads = jax.ShapeDtypeStruct((heads, head_size, row_count), jnp.float32)
    return pl.pallas_call(
        lambda *refs: attend_grad_kernel(scale, *refs),
        grid=(heads, row_count // block),
        in_specs=[part, full, full, own, every, log, part, part],
        out_specs=[part, full, full],
        out_shape=[grads, grads, grads],
        name="attend_grads",
    )(query_cols, key_cols, value_cols, seg_col, seg_row, log_total, grad_cols, attended_cols)


def weight_grads_kernel(bounds, *refs):
    gain_ref, out_ref = refs[-2:]
    for i in range(3):
        out_ref[:, bounds[i] : bounds[i] + refs[2 * i + 1].shape[1]] = lax.dot_general(
            refs[2 * i][...],
            refs[2 * i + 1][...],
            (((0,), (0,)), ((), ())),
            preferred_element_type=jnp.float32,
        ).astype(jnp.bfloat16)
    out_ref[:, bounds[3] : bounds[3] + LANES] = gain_ref[...]


def weight_grads(pairs, gain_block, bounds, total):
    tok_count, width = pairs[0][0].shape
    rows = min(LANES, width)
    in_specs = []
    operands = []
    for left, right in pairs:
        in_specs.append(pl.BlockSpec((tok_count, rows), lambda r: (0, r)))
        in_specs.append(pl.BlockSpec(right.shape, lambda r: (0, 0)))
        operands += [left, right]
    in_specs.append(pl.BlockSpec((rows, LANES), lambda r: (r, 0)))
    return pl.pallas_call(
        lambda *refs: weight_grads_kernel(bounds, *refs),
        grid=(width // rows,),
        in_specs=in_specs,
        out_specs=pl.BlockSpec((rows, total), lambda r: (r, 0)),
        out_shape=jax.ShapeDtypeStruct((width, total), jnp.bfloat16),
        name="weight_grads",
    )(*operands, gain_block)


def body(
    ctx_size,
    fsdp_size,
    inputs,
    segment_ids,
    gain_attn,
    w_qkv,
    w_out_attn,
    gain_mlp,
    w_in,
    w_out_mlp,
    cotangent,
):
    tok_count, width = inputs.shape[1:]
    heads = HEADS
    head_size = HD
    scale = 1.0 / math.sqrt(head_size)
    everyone = ("ctx", "fsdp")
    hidden_units = w_out_mlp.shape[0]
    row_count = ctx_size * tok_count
    devices = ctx_size * fsdp_size
    own_heads = heads // ctx_size
    own_width = own_heads * head_size
    weight_rows = w_qkv.shape[0]

    seg_block = jnp.pad(segment_ids.astype(jnp.bfloat16), ((0, SEG_ROWS - 1), (0, width - tok_count)))
    gathered = lax.all_to_all(
        jnp.broadcast_to(
            jnp.concatenate([inputs[0], seg_block], axis=0),
            (ctx_size, tok_count + SEG_ROWS, width),
        ),
        "ctx",
        0,
        0,
        tiled=True,
    )

    qkv_parts = jnp.transpose(
        w_qkv.reshape(weight_rows, 3, ctx_size, own_width), (2, 0, 1, 3)
    ).reshape(ctx_size, weight_rows, 3 * own_width)
    gains_own = jnp.pad(jnp.stack([gain_attn, gain_mlp], axis=1), ((0, 0), (0, LANES - 2)))
    qkv_parts = jnp.concatenate(
        [qkv_parts, jnp.broadcast_to(gains_own, (ctx_size, weight_rows, LANES))], axis=2
    )
    qkv_parts = jnp.broadcast_to(
        qkv_parts[:, None], (ctx_size, fsdp_size, weight_rows, 3 * own_width + LANES)
    ).reshape(devices, weight_rows, 3 * own_width + LANES)
    qkv_got = lax.all_to_all(qkv_parts, everyone, 0, 0, tiled=True).reshape(
        devices * weight_rows, 3 * own_width + LANES
    )
    qkv_mine = qkv_got[:, : 3 * own_width]
    gains = qkv_got[:, 3 * own_width : 3 * own_width + 2].astype(jnp.float32).T
    gain_first = gains[0]
    gain_second = gains[1]

    rest_own = jnp.concatenate([w_out_attn, w_in, w_out_mlp.T], axis=1)
    rest_full = lax.all_gather(rest_own, everyone, axis=0, tiled=True)
    attn_full = rest_full[:, :width]
    in_full = rest_full[:, width : width + 2 * hidden_units]
    mlp_turned = rest_full[:, width + 2 * hidden_units :]

    seg_row = gathered[:, tok_count, :tok_count].reshape(1, row_count).astype(jnp.float32)
    seg_col = seg_row.reshape(row_count, 1)
    row_tokens = gathered[:, :tok_count].reshape(row_count, width).astype(jnp.float32)
    row_normed, unused = layer_norm(row_tokens)
    row_normed_attn = (row_normed * gain_first).astype(jnp.bfloat16)
    tokens = inputs[0].astype(jnp.float32)
    normed_one, scale_one = layer_norm(tokens)

    projected_cols = jnp.einsum(
        "de,td->et", qkv_mine, row_normed_attn, preferred_element_type=jnp.float32
    ).reshape(3, own_heads, head_size, row_count)
    positions = jnp.arange(row_count, dtype=jnp.int32).astype(jnp.float32)
    cosine, sine = rope_columns(positions, head_size)
    query_cols = rotate_cols(projected_cols[0], cosine, sine).astype(jnp.bfloat16)
    key_cols = rotate_cols(projected_cols[1], cosine, sine).astype(jnp.bfloat16)
    value_cols = projected_cols[2].astype(jnp.bfloat16)
    row_attended, log_total = attend(query_cols, key_cols, value_cols, seg_col, seg_row, scale)

    attended = lax.all_to_all(
        row_attended.reshape(own_width, row_count).T.reshape(ctx_size, tok_count, own_width),
        "ctx",
        0,
        0,
        tiled=True,
    )
    attended = jnp.transpose(attended, (1, 0, 2)).reshape(tok_count, width)
    residual = tokens + jnp.dot(attended, attn_full, preferred_element_type=jnp.float32)
    normed_two, scale_two = layer_norm(residual)
    normed_mlp = (normed_two * gain_second).astype(jnp.bfloat16)
    expanded = jnp.dot(normed_mlp, in_full, preferred_element_type=jnp.float32)
    pre_act = expanded[:, :hidden_units]
    gate_part = expanded[:, hidden_units:]
    activated = jax.nn.gelu(pre_act, approximate=False)
    product = (activated * gate_part).astype(jnp.bfloat16)
    block_out = (
        residual
        + jnp.einsum("tf,df->td", product, mlp_turned, preferred_element_type=jnp.float32)
    ).astype(jnp.bfloat16)
    grad_out = cotangent[0]
    grad_product = jnp.einsum("td,df->tf", grad_out, mlp_turned, preferred_element_type=jnp.float32)
    grad_expanded = jnp.concatenate(
        [grad_product * gate_part * gelu_slope(pre_act), grad_product * activated], axis=1
    ).astype(jnp.bfloat16)
    grad_normed_mlp = jnp.einsum(
        "tf,df->td", grad_expanded, in_full, preferred_element_type=jnp.float32
    )
    grad_gain_two = jnp.sum(grad_normed_mlp * normed_two, axis=0)
    grad_residual = grad_out.astype(jnp.float32) + norm_back(
        grad_normed_mlp * gain_second, normed_two, scale_two
    )
    residual_half = grad_residual.astype(jnp.bfloat16)
    gain_block = jnp.pad(grad_gain_two[:, None], ((0, 0), (0, LANES - 1))).astype(jnp.bfloat16)
    weight_sums = lax.psum_scatter(
        weight_grads(
            (
                (attended, residual_half),
                (normed_mlp, grad_expanded),
                (grad_out, product),
            ),
            gain_block,
            (0, width, width + 2 * hidden_units + LANES, width + 2 * hidden_units),
            width + 3 * hidden_units + LANES,
        ),
        everyone,
        scatter_dimension=0,
        tiled=True,
    ).astype(jnp.float32)
    grad_attended = jnp.einsum(
        "te,de->td", residual_half, attn_full, preferred_element_type=jnp.float32
    ).astype(jnp.bfloat16)
    row_grad = lax.all_to_all(
        jnp.transpose(grad_attended.reshape(tok_count, ctx_size, own_width), (1, 0, 2)),
        "ctx",
        0,
        0,
        tiled=True,
    )
    row_grad_cols = row_grad.reshape(row_count, own_width).T.reshape(
        own_heads, head_size, row_count
    )
    grad_query, grad_key, grad_value = attend_grads(
        query_cols,
        key_cols,
        value_cols,
        seg_col,
        seg_row,
        log_total,
        row_grad_cols,
        row_attended,
        scale,
    )
    grad_proj_cols = (
        jnp.stack(
            [
                unrotate_cols(grad_query, cosine, sine),
                unrotate_cols(grad_key, cosine, sine),
                grad_value,
            ],
            axis=0,
        )
        .astype(jnp.bfloat16)
        .reshape(3 * own_width, row_count)
    )
    row_grad_normed = jnp.einsum(
        "de,et->td", qkv_mine, grad_proj_cols, preferred_element_type=jnp.float32
    )
    grad_gain_part = jnp.sum(row_grad_normed * row_normed, axis=0)
    grad_normed_attn = jnp.sum(
        lax.all_to_all(
            row_grad_normed.astype(jnp.bfloat16).reshape(ctx_size, tok_count, width),
            "ctx",
            0,
            0,
            tiled=True,
        ).astype(jnp.float32),
        axis=0,
    )
    qkv_terms = jnp.concatenate(
        [
            jnp.einsum(
                "td,et->de", row_normed_attn, grad_proj_cols, preferred_element_type=jnp.float32
            ).astype(jnp.bfloat16),
            jnp.pad(grad_gain_part[:, None], ((0, 0), (0, LANES - 1))).astype(jnp.bfloat16),
        ],
        axis=1,
    ).reshape(devices, weight_rows, 3 * own_width + LANES)
    qkv_sums = jnp.sum(
        lax.all_to_all(qkv_terms, everyone, 0, 0, tiled=True)
        .reshape(ctx_size, fsdp_size, weight_rows, 3 * own_width + LANES)
        .astype(jnp.float32),
        axis=1,
    )
    grad_qkv_rows = jnp.transpose(
        qkv_sums[:, :, : 3 * own_width].reshape(ctx_size, weight_rows, 3, own_width), (1, 2, 0, 3)
    ).reshape(weight_rows, 3 * width)
    gain_sum_one = jnp.sum(qkv_sums[:, :, 3 * own_width], axis=0)
    grad_tokens = (
        grad_residual + norm_back(grad_normed_attn * gain_first, normed_one, scale_one)
    ).astype(jnp.bfloat16)
    grad_attn_rows = weight_sums[:, :width]
    grad_in_rows = weight_sums[:, width : width + 2 * hidden_units]
    grad_mlp_cols = weight_sums[:, width + 2 * hidden_units + LANES :].T
    gain_sum_two = weight_sums[:, width + 2 * hidden_units]
    return (
        block_out[None],
        grad_tokens[None],
        grad_qkv_rows,
        grad_attn_rows,
        grad_in_rows,
        grad_mlp_cols,
        gain_sum_one,
        gain_sum_two,
    )


def solution(mesh):
    in_specs = (
        P("fsdp", "ctx", None),
        P("fsdp", "ctx"),
        P(("ctx", "fsdp")),
        P(("ctx", "fsdp"), None),
        P(("ctx", "fsdp"), None),
        P(("ctx", "fsdp")),
        P(("ctx", "fsdp"), None),
        P(None, ("ctx", "fsdp")),
        P("fsdp", "ctx", None),
    )
    out_specs = (
        P("fsdp", "ctx", None),
        P("fsdp", "ctx", None),
        P(("ctx", "fsdp"), None),
        P(("ctx", "fsdp"), None),
        P(("ctx", "fsdp"), None),
        P(None, ("ctx", "fsdp")),
        P(("ctx", "fsdp")),
        P(("ctx", "fsdp")),
    )
    step = functools.partial(body, mesh.shape["ctx"], mesh.shape["fsdp"])
    return jax.shard_map(step, mesh=mesh, in_specs=in_specs, out_specs=out_specs, check_vma=False)
```
